32 devices in a mesh: dp: 8 (over z, x), ctx: 4 (over y, core).
Axes of the slice: x: 2, y: 2, z: 4, core: 2. Of those that a mesh axis runs over, the one named last changes fastest.
Arguments:
- features: bfloat16 [4096, 4096], P(('dp', 'ctx')), may hold values from -6 to 6
- gate_in: bfloat16 [4096, 4096], P(('dp', 'ctx')), may hold values from -6 to 6
- gate_out: bfloat16 [4096, 4096], P(('dp', 'ctx')), may hold values from -6 to 6
- value_weight: bfloat16 [4096, 4096], P('dp', 'ctx'), may hold values from -0.09375 to 0.09375
- short_taps: float32 [3, 7, 4096], replicated, may hold values from -2 to 2
- medium_taps: bfloat16 [128, 256], replicated, may hold values from -0.5 to 0.5
- cotangent: bfloat16 [4096, 4096], P(('dp', 'ctx')), may hold values from -6 to 6
Outputs:
- layer_out: bfloat16 [4096, 4096], P(('dp', 'ctx'))
- grad_features: bfloat16 [4096, 4096], P(('dp', 'ctx'))
- grad_gate_in: bfloat16 [4096, 4096], P(('dp', 'ctx'))
- grad_gate_out: bfloat16 [4096, 4096], P(('dp', 'ctx'))
- grad_weight: bfloat16 [4096, 4096], P('dp', 'ctx')
- grad_short: float32 [3, 7, 4096], P(None, None, 'ctx')
- grad_medium: float32 [128, 256], P(None, 'ctx')
The draws below stay inside these ranges and needn't reach their ends.
All inputs are finite; a program needn't handle non-finite values.
Results may differ from the reference program's by a relative error of at most 0.025.
Values may be sent and summed in bfloat16 or wider, within the bound.
A program may use at most 256 MiB of HBM per device.

```python
import math
import jax
import jax.numpy as jnp
from jax import lax

D = 4096
GROUP_WIDTH = 16
GROUPS = 256
KS = 7
FILT = 128
LEN = 512
WINDOWS = 8
TOKENS = 4096
N_CTX = 4


def strengthened(array, rng, source, target, parts, factor):
    owner, partner = [(jnp.arange(array.shape[dim]) // (array.shape[dim] // parts)).reshape([-1 if axis == dim else 1 for axis in range(array.ndim)]) for dim in (source, target)]
    chosen = jax.random.permutation(rng, parts)[partner]
    strong = (owner == chosen) | (owner == (partner + parts // 2) % parts)
    return jnp.where(strong, factor * array, array)


def shard_levels(key, dims, split, smallest, largest):
    factor_of = 1.0
    for axis_at, parts in split:
        heights = jax.random.uniform(jax.random.fold_in(jax.random.fold_in(key, 6), axis_at), (parts,), jnp.float32, smallest / len(split), largest / len(split))
        factor_of = factor_of * jnp.repeat(jnp.exp(heights), dims[axis_at] // parts).reshape((-1,) + (1,) * (len(dims) - 1 - axis_at))
    return factor_of


def bell_draw(key, shape, scale, bound, cuts=(), kind=jnp.bfloat16):
    drawn = jax.random.normal(key, shape, jnp.float32) * scale
    if len(cuts) > 0:
        drawn = shard_levels(key, shape, cuts, -0.22, 0.18) * drawn
    return jnp.clip(drawn, min=-bound, max=bound).astype(kind)


def bell_draw_with(stream_key, dims, spread, bound, shards, heavy, held_as=jnp.bfloat16):
    result = spread * jax.random.normal(stream_key, dims, jnp.float32)
    if shards:
        result = result * shard_levels(stream_key, dims, shards, -0.22, 0.18)
    return jnp.clip(strengthened(result, jax.random.fold_in(stream_key, 3), *heavy), -bound, bound).astype(held_as)


def setup_inputs(seed: int = 0) -> dict:
    arg_keys = jax.random.split(jax.random.key(seed), 8)
    return {
        "features": bell_draw_with(arg_keys[0], (TOKENS, D), 1.0, 6.0, ((0, 32),), (0, 1, 32, 2.75)),
        "gate_in": bell_draw(arg_keys[1], (TOKENS, D), 1.0, 6.0, ((0, 32),)),
        "gate_out": bell_draw(arg_keys[2], (TOKENS, D), 1.0, 6.0, ((0, 32),)),
        "value_weight": bell_draw(arg_keys[3], (D, D), D ** -0.5, 0.09375, ((0, 8), (1, 4))),
        "short_taps": bell_draw(arg_keys[4], (3, KS, D), KS ** -0.5, 2.0, (), jnp.float32),
        "medium_taps": bell_draw(arg_keys[5], (FILT, GROUPS), FILT ** -0.5, 0.5),
        "cotangent": bell_draw(arg_keys[6], (TOKENS, D), 1.0, 6.0, ((0, 32),)),
    }


def causal_conv(stream, conv_taps, prior_rows):
    conv_edge = conv_taps.shape[0] - 1
    row_count = stream.shape[0]
    extended = jnp.concatenate([prior_rows, stream], axis=0)
    running = conv_taps[0] * extended[conv_edge:conv_edge + row_count]
    for shift_back in range(1, conv_edge + 1):
        running = running + conv_taps[shift_back] * extended[conv_edge - shift_back:conv_edge - shift_back + row_count]
    return running

def conv_back(gradient, conv_taps, later_rows):
    conv_edge = conv_taps.shape[0] - 1
    row_count = gradient.shape[0]
    extended = jnp.concatenate([gradient, later_rows], axis=0)
    running = conv_taps[0] * extended[:row_count]
    for ahead in range(1, conv_edge + 1):
        running = running + conv_taps[ahead] * extended[ahead:ahead + row_count]
    return running

def conv_taps_grad(gradient, stream, prior_rows):
    conv_edge = prior_rows.shape[0]
    row_count = stream.shape[0]
    extended = jnp.concatenate([prior_rows, stream], axis=0)
    return jnp.stack([lax.optimization_barrier(jnp.sum(gradient * extended[conv_edge - shift_back:conv_edge - shift_back + row_count], axis=0)) for shift_back in range(conv_edge + 1)])

def toeplitz_table(medium):
    filter_span, group_count = medium.shape
    padded = jnp.concatenate([jnp.zeros((1, group_count), medium.dtype), medium[::-1], jnp.zeros((filter_span, group_count), medium.dtype)], axis=0)
    tiled = jnp.tile(padded.T, (1, filter_span))
    return tiled[:, :2 * filter_span * filter_span].reshape(group_count, filter_span, 2 * filter_span)

def fold_table(grad_table):
    group_count, filter_span, double_span = grad_table.shape
    flat = grad_table.reshape(group_count, filter_span * double_span)
    flat = jnp.concatenate([flat, jnp.zeros((group_count, filter_span), grad_table.dtype)], axis=1)
    summed = lax.optimization_barrier(jnp.sum(flat.reshape(group_count, filter_span, double_span + 1), axis=1))
    return summed[:, 1:filter_span + 1][:, ::-1].T

def apply_toeplitz(toeplitz, before, product):
    group_count, filter_span = (toeplitz.shape[0], toeplitz.shape[1])
    row_count, channels = product.shape
    block_shape = (row_count // filter_span, filter_span, group_count, channels // group_count)
    extended = jnp.concatenate([before, product], axis=0)
    lower_half = extended[:row_count].reshape(block_shape)
    upper_half = extended[filter_span:].reshape(block_shape)
    window = jnp.concatenate([lower_half, upper_half], axis=1)
    filtered = jnp.einsum('gij,bjgs->bigs', toeplitz.astype(jnp.float32), window.astype(jnp.float32))
    return (filtered.reshape(row_count, channels), window)

def toeplitz_back(toeplitz, medium, grad_filtered, later_rows, window):
    group_count, filter_span = (toeplitz.shape[0], toeplitz.shape[1])
    row_count, channels = grad_filtered.shape
    block_shape = (row_count // filter_span, filter_span, group_count, channels // group_count)
    current = grad_filtered.reshape(block_shape).astype(jnp.float32)
    following = jnp.concatenate([grad_filtered[filter_span:], later_rows], axis=0).reshape(block_shape).astype(jnp.float32)
    table = toeplitz.astype(jnp.float32)
    grad_product = jnp.einsum('gij,bigs->bjgs', table[:, :, filter_span:], current) + jnp.einsum('gij,bigs->bjgs', table[:, :, :filter_span], following)
    grad_table = jnp.einsum('bigs,bjgs->gij', current, window.astype(jnp.float32))
    return (grad_product.reshape(row_count, channels), fold_table(grad_table))

def reference(features, gate_in, gate_out, value_weight, short_taps, medium_taps, cotangent):
    row_scale = 1.0 / math.sqrt(TOKENS)
    group_scale = 1.0 / math.sqrt(TOKENS * GROUP_WIDTH)
    toeplitz = toeplitz_table(medium_taps)
    zero_rim = jnp.zeros((KS - 1, D), jnp.bfloat16)
    zero_span = jnp.zeros((FILT, D), jnp.bfloat16)
    zero_after = jnp.zeros((KS - 1, D), jnp.float32)
    weight_blocks = value_weight.reshape(D, N_CTX, D // N_CTX).astype(jnp.float32)

    def one_window(state_sums, pieces):
        weight_sum, short_sum, medium_sum = state_sums
        window_features, window_in, window_out, window_cot = pieces
        values = jnp.dot(window_features, value_weight, preferred_element_type=jnp.float32).astype(jnp.bfloat16)
        streams = (window_in, window_out, values)
        convs = [causal_conv(streams[index], short_taps[index], zero_rim) for index in range(3)]
        product = (convs[0] * convs[2]).astype(jnp.bfloat16)
        filtered, window = apply_toeplitz(toeplitz, zero_span, product)
        layer_out = (convs[1] * filtered).astype(jnp.bfloat16)
        grad_filtered = (window_cot * convs[1]).astype(jnp.bfloat16)
        grad_product, medium_grad = toeplitz_back(toeplitz, medium_taps, grad_filtered, zero_span, window)
        grad_convs = (grad_product * convs[2], window_cot * filtered, grad_product * convs[0])
        grad_streams = [conv_back(grad_convs[index], short_taps[index], zero_after) for index in range(3)]
        short_grad = jnp.stack([conv_taps_grad(grad_convs[index], streams[index], zero_rim) for index in range(3)])
        grad_values = grad_streams[2].astype(jnp.bfloat16)
        window_term = lax.dot_general(window_features, grad_values, (((0,), (0,)), ((), ())), preferred_element_type=jnp.float32) * row_scale
        window_term = lax.optimization_barrier(window_term.astype(jnp.bfloat16)).astype(jnp.float32)
        value_blocks = grad_values.reshape(LEN, N_CTX, D // N_CTX).astype(jnp.float32)
        block_terms = jnp.einsum('tjc,djc->jtd', value_blocks, weight_blocks)
        block_terms = lax.optimization_barrier(block_terms.astype(jnp.bfloat16)).astype(jnp.float32)
        grad_features = lax.optimization_barrier(jnp.sum(block_terms, axis=0)).astype(jnp.bfloat16)
        new_sums = (weight_sum + window_term, short_sum + short_grad * row_scale, medium_sum + medium_grad * group_scale)
        return (new_sums, (layer_out, grad_features, grad_streams[0].astype(jnp.bfloat16), grad_streams[1].astype(jnp.bfloat16)))
    start_sums = (jnp.zeros((D, D), jnp.float32), jnp.zeros((3, KS, D), jnp.float32), jnp.zeros((FILT, GROUPS), jnp.float32))
    stacked = (features.reshape(WINDOWS, LEN, D), gate_in.reshape(WINDOWS, LEN, D), gate_out.reshape(WINDOWS, LEN, D), cotangent.reshape(WINDOWS, LEN, D))
    final_sums, outputs = lax.scan(one_window, start_sums, stacked)
    layer_out, grad_features, grad_gate_in, grad_gate_out = [piece.reshape(TOKENS, D) for piece in outputs]
    return (layer_out, grad_features, grad_gate_in, grad_gate_out, final_sums[0].astype(jnp.bfloat16), final_sums[1], final_sums[2])
```

```python
import functools
import math

import jax
import jax.numpy as jnp
from jax import lax
from jax.experimental import pallas as pl
from jax.experimental.pallas import tpu as pltpu
from jax.sharding import PartitionSpec as P

MESH = pl.DeviceIdType.MESH
ANY = pl.BlockSpec(memory_space=pl.ANY)
LANES = 128
CHUNK = 64


def greet(dp, ctx):
    me_dp, me_ctx = lax.axis_index("dp"), lax.axis_index("ctx")
    barrier = pltpu.get_barrier_semaphore()
    for step in range(1, dp):
        pl.semaphore_signal(
            barrier, inc=1, device_id=(lax.rem(me_dp + step, dp), me_ctx), device_id_type=MESH
        )
    for step in range(1, ctx):
        pl.semaphore_signal(
            barrier, inc=1, device_id=(me_dp, lax.rem(me_ctx + step, ctx)), device_id_type=MESH
        )
    pl.semaphore_wait(barrier, dp + ctx - 2)


def send(src, dst, send_sem, recv_sem, device):
    return pltpu.make_async_remote_copy(
        src_ref=src,
        dst_ref=dst,
        send_sem=send_sem,
        recv_sem=recv_sem,
        device_id=device,
        device_id_type=MESH,
    )


def gather_kernel(
    dp, ctx, pair,
    features, gate_in, gate_out, cot, weight,
    window, block_in, block_out, block_cot, full,
    local_sem, ctx_send, ctx_recv, right_send, left_send, pair_send, full_recv,
):
    me_dp, me_ctx = lax.axis_index("dp"), lax.axis_index("ctx")
    line = dp // pair
    at, side = me_dp // pair, lax.rem(me_dp, pair)
    rows = features.shape[0]
    cols, depth = weight.shape[1], weight.shape[0]
    greet(dp, ctx)

    def block(index):
        return full.at[pl.ds(pl.multiple_of(index * depth, depth), depth)]

    def push(src, index, sem, to):
        return send(src, block(index), sem, full_recv.at[index], (to, me_ctx))

    def others(index, src):
        if pair == 2:
            push(src, index, pair_send.at[index // pair], at * pair + 1 - side).start()

    @pl.when(at + 1 < line)
    def _():
        push(weight, me_dp, right_send.at[at], me_dp + pair).start()

    @pl.when(at > 0)
    def _():
        push(weight, me_dp, left_send.at[at], me_dp - pair).start()

    others(me_dp, weight)

    mine = pl.ds(pl.multiple_of(me_ctx * rows, rows), rows)
    streams = ((gate_in, block_in), (gate_out, block_out), (cot, block_cot))
    copies = []
    for which, (src, dst) in enumerate(((features, window),) + streams):
        for step in range(1, ctx):
            peer = lax.rem(me_ctx + step, ctx)
            part = src if which == 0 else src.at[:, pl.ds(pl.multiple_of(peer * cols, cols), cols)]
            copies.append(
                send(
                    part, dst.at[mine], ctx_send.at[which, step], ctx_recv.at[which, step],
                    (me_dp, peer),
                )
            )
            copies[-1].start()
    stays = [pltpu.make_async_copy(weight, block(me_dp), local_sem.at[4])]
    stays.append(pltpu.make_async_copy(features, window.at[mine], local_sem.at[0]))
    for which, (src, dst) in enumerate(streams):
        part = src.at[:, pl.ds(pl.multiple_of(me_ctx * cols, cols), cols)]
        stays.append(pltpu.make_async_copy(part, dst.at[mine], local_sem.at[which + 1]))
    for copy in stays:
        copy.start()

    def arrived(index):
        push(block(index), index, right_send.at[0], me_dp).wait_recv()

    for far in range(1, line):
        @pl.when(at - far >= 0)
        def _():
            index = me_dp - far * pair
            arrived(index)

            @pl.when(at + 1 < line)
            def _():
                push(block(index), index, right_send.at[at - far], me_dp + pair).start()

            others(index, block(index))

        @pl.when(at + far < line)
        def _():
            index = me_dp + far * pair
            arrived(index)

            @pl.when(at > 0)
            def _():
                push(block(index), index, left_send.at[at + far], me_dp - pair).start()

            others(index, block(index))

    for copy in copies:
        copy.wait()
    for copy in stays:
        copy.wait()
    for spot in range(line):
        if pair == 2:
            arrived(spot * pair + 1 - side)
            push(weight, me_dp, pair_send.at[spot], me_dp).wait_send()

        @pl.when((at + 1 < line) & (spot <= at))
        def _():
            push(weight, me_dp, right_send.at[spot], me_dp).wait_send()

        @pl.when((at > 0) & (spot >= at))
        def _():
            push(weight, me_dp, left_send.at[spot], me_dp).wait_send()


def gather_all(dp, ctx, features, gate_in, gate_out, cot, weight):
    pair = 2 if dp % 2 == 0 else 1
    rows, channels = features.shape
    depth, cols = weight.shape
    shapes = [(rows * ctx, channels)] + [(rows * ctx, cols)] * 3 + [(depth * dp, cols)]
    dma = pltpu.SemaphoreType.DMA
    line = dp // pair
    return pl.pallas_call(
        functools.partial(gather_kernel, dp, ctx, pair),
        out_shape=[jax.ShapeDtypeStruct(shape, jnp.bfloat16) for shape in shapes],
        in_specs=[ANY] * 5,
        out_specs=[ANY] * 5,
        scratch_shapes=[
            dma((5,)), dma((4, ctx)), dma((4, ctx)), dma((line,)), dma((line,)), dma((line,)),
            dma((dp,)),
        ],
        compiler_params=pltpu.CompilerParams(collective_id=0, has_side_effects=True),
    )(features, gate_in, gate_out, cot, weight)


def scatter_kernel(
    dp, ctx, pair,
    grad_weight, terms, layer, first, second, small,
    weight_out, terms_out, layer_out, first_out, second_out, small_out,
    held, from_pair, from_left, from_right,
    local_sem, held_sem, ctx_send, ctx_recv, small_send, small_recv,
    pair_send, pair_recv, right_send, left_recv, left_send, right_recv, out_sem,
):
    me_dp, me_ctx = lax.axis_index("dp"), lax.axis_index("ctx")
    line = dp // pair
    at, side = me_dp // pair, lax.rem(me_dp, pair)
    rows, cols = layer_out.shape[0], layer.shape[1]
    depth = weight_out.shape[0]
    greet(dp, ctx)

    def block(index):
        return grad_weight.at[pl.ds(pl.multiple_of(index * depth, depth), depth)]

    def keep(spot):
        return pltpu.make_async_copy(block(spot * pair + side), held.at[spot], held_sem.at[spot])

    def swap(spot):
        return send(
            block(spot * pair + 1 - side), from_pair.at[spot], pair_send.at[spot],
            pair_recv.at[spot], (at * pair + 1 - side, me_ctx),
        )

    def to_right(spot):
        return send(
            held.at[spot], from_left.at[spot], right_send.at[spot], left_recv.at[spot],
            (me_dp + pair, me_ctx),
        )

    def to_left(spot):
        return send(
            held.at[spot], from_right.at[spot], left_send.at[spot], right_recv.at[spot],
            (me_dp - pair, me_ctx),
        )

    def begin(spot):
        if pair == 2:
            swap(spot).start()
        keep(spot).start()

    for far in range(line - 1, 0, -1):
        pl.when(at + far < line)(functools.partial(begin, at + far))
        pl.when(at - far >= 0)(functools.partial(begin, at - far))
    begin(at)

    copies = []
    mine = pl.ds(pl.multiple_of(me_ctx * cols, cols), cols)
    for step in range(1, dp):
        peer = lax.rem(me_dp + step, dp)
        copies.append(
            send(small, small_out.at[me_dp], small_send.at[step], small_recv.at[step], (peer, me_ctx))
        )
    outs = ((layer, layer_out), (first, first_out), (second, second_out))
    for which, (src, dst) in enumerate(((terms, terms_out),) + outs):
        for step in range(1, ctx):
            peer = lax.rem(me_ctx + step, ctx)
            copies.append(
                send(
                    src.at[pl.ds(pl.multiple_of(peer * rows, rows), rows)],
                    dst.at[me_ctx] if which == 0 else dst.at[:, mine],
                    ctx_send.at[which, step], ctx_recv.at[which, step], (me_dp, peer),
                )
            )
        part = src.at[pl.ds(pl.multiple_of(me_ctx * rows, rows), rows)]
        copies.append(
            pltpu.make_async_copy(
                part, dst.at[me_ctx] if which == 0 else dst.at[:, mine], local_sem.at[which]
            )
        )
    copies.append(pltpu.make_async_copy(small, small_out.at[me_dp], local_sem.at[4]))
    for copy in copies:
        copy.start()

    span = 32

    def add(spot, source):
        def body(step, carry):
            part = pl.ds(pl.multiple_of(step * span, span), span)
            held[spot, part] = (
                held[spot, part].astype(jnp.float32) + source[spot, part].astype(jnp.float32)
            ).astype(jnp.bfloat16)
            return carry

        lax.fori_loop(0, depth // span, body, 0)

    def ready(spot):
        keep(spot).wait()
        if pair == 2:
            swap(spot).wait_recv()
            add(spot, from_pair)

    def go_right(spot):
        ready(spot)

        @pl.when(at > 0)
        def _():
            to_right(spot).wait_recv()
            add(spot, from_left)

        to_right(spot).start()

    def go_left(spot):
        ready(spot)

        @pl.when(at + 1 < line)
        def _():
            to_left(spot).wait_recv()
            add(spot, from_right)

        to_left(spot).start()

    for far in range(line - 1, 0, -1):
        pl.when(at + far < line)(functools.partial(go_right, at + far))
        pl.when(at - far >= 0)(functools.partial(go_left, at - far))
    ready(at)

    @pl.when(at > 0)
    def _():
        to_right(at).wait_recv()
        add(at, from_left)

    @pl.when(at + 1 < line)
    def _():
        to_left(at).wait_recv()
        add(at, from_right)

    result = pltpu.make_async_copy(held.at[at], weight_out, out_sem)
    result.start()
    for copy in copies:
        copy.wait()
    for spot in range(line):
        if pair == 2:
            swap(spot).wait_send()
        pl.when(spot > at)(lambda spot=spot: to_right(spot).wait_send())
        pl.when(spot < at)(lambda spot=spot: to_left(spot).wait_send())
    result.wait()


def scatter_all(dp, ctx, grad_weight, terms, layer, first, second, small):
    pair = 2 if dp % 2 == 0 else 1
    line = dp // pair
    length, cols = layer.shape
    rows, channels, depth = length // ctx, terms.shape[1], grad_weight.shape[0] // dp
    shapes = [(depth, cols), (ctx, rows, channels)] + [(rows, channels)] * 3 + [(dp,) + small.shape]
    dma = pltpu.SemaphoreType.DMA
    slots = pltpu.VMEM((line, depth, cols), jnp.bfloat16)
    return pl.pallas_call(
        functools.partial(scatter_kernel, dp, ctx, pair),
        out_shape=[jax.ShapeDtypeStruct(shape, jnp.bfloat16) for shape in shapes],
        in_specs=[ANY] * 6,
        out_specs=[ANY] * 6,
        scratch_shapes=[slots] * 4
        + [dma((5,)), dma((line,)), dma((4, ctx)), dma((4, ctx)), dma((dp,)), dma((dp,))]
        + [dma((line,))] * 6
        + [dma],
        compiler_params=pltpu.CompilerParams(
            collective_id=1, has_side_effects=True, vmem_limit_bytes=40 * 2**20
        ),
    )(grad_weight, terms, layer, first, second, small)


def mixer_kernel(
    group_width,
    gate_in, gate_out, values, cot, taps, ahead, behind,
    layer, grad_in, grad_out, grad_values, grad_short, grad_medium,
    streams, convs, grads, product, grad_filtered, table, back, filtered, grad_product,
):
    length = gate_in.shape[0]
    span = table.shape[1] // 2
    groups = LANES // group_width
    edge = taps.shape[1]
    f32, bf16 = jnp.float32, jnp.bfloat16
    streams[:, :8] = jnp.zeros((3, 8, LANES), f32)
    grads[:, length:] = jnp.zeros((3, 8, LANES), f32)
    product[:span] = jnp.zeros((span, LANES), bf16)
    grad_filtered[length:] = jnp.zeros((span, LANES), bf16)
    for index, stream in enumerate((gate_in, gate_out, values)):
        streams[index, 8:] = stream[...].astype(f32)

    for source, target in ((ahead, table), (behind, back)):
        for group in range(groups):
            rows = jnp.broadcast_to(source[group : group + 1], (8, 2 * span))
            offset = lax.broadcasted_iota(jnp.int32, (8, 2 * span), 0)
            for bit in (1, 2, 4):
                rows = jnp.where((offset & bit) != 0, pltpu.roll(rows, bit, 1), rows)
            height = 8
            while height < span:
                rows = jnp.concatenate([rows, pltpu.roll(rows, height, 1)], axis=0)
                height *= 2
            target[group * span : (group + 1) * span] = rows.astype(bf16)

    for base in range(0, length, CHUNK):
        part = slice(base, base + CHUNK)
        conv = []
        for index in range(3):
            running = taps[index, 0:1] * streams[index, 8 + base : 8 + base + CHUNK]
            for shift in range(1, edge):
                start = 8 + base - shift
                running = running + taps[index, shift : shift + 1] * streams[index, start : start + CHUNK]
            conv.append(running)
            convs[index, part] = running
        product[span + base : span + base + CHUNK] = (conv[0] * conv[2]).astype(bf16)
        grad_filtered[part] = (cot[part].astype(f32) * conv[1]).astype(bf16)

    owner = lax.broadcasted_iota(jnp.int32, (span, LANES), 1) // group_width
    for base in range(0, length, span):
        near = product[base : base + 2 * span]
        for matrix, window, target in (
            (table, near, filtered),
            (back, grad_filtered[base : base + 2 * span], grad_product),
        ):
            chosen = None
            for group in range(groups):
                out = jnp.dot(
                    matrix[group * span : (group + 1) * span], window, preferred_element_type=f32
                )
                chosen = out if chosen is None else jnp.where(owner == group, out, chosen)
            target[base : base + span] = chosen

    for group in range(groups):
        total = None
        for base in range(0, length, span):
            current = grad_filtered[base : base + span].astype(f32)
            current = jnp.where(owner == group, current, 0.0).astype(bf16)
            term = lax.dot_general(
                current, product[base : base + 2 * span], (((1,), (1,)), ((), ())),
                preferred_element_type=f32,
            )
            total = term if total is None else total + term
        height = span // 2
        while height >= 8:
            total = total[:height] + pltpu.roll(total[height:], 2 * span - height, 1)
            height //= 2
        offset = lax.broadcasted_iota(jnp.int32, (8, 2 * span), 0)
        for bit in (1, 2, 4):
            total = jnp.where((offset & bit) != 0, pltpu.roll(total, 2 * span - bit, 1), total)
        grad_medium[group : group + 1] = jnp.sum(total, axis=0, keepdims=True)

    for base in range(0, length, CHUNK):
        part = slice(base, base + CHUNK)
        kept = filtered[part]
        gradient = grad_product[part]
        layer[part] = (convs[1, part] * kept).astype(bf16)
        grads[0, part] = gradient * convs[2, part]
        grads[1, part] = cot[part].astype(f32) * kept
        grads[2, part] = gradient * convs[0, part]

    outs = (grad_in, grad_out, grad_values)
    for index in range(3):
        tap_sums = [jnp.zeros((8, LANES), f32) for _ in range(edge)]
        for base in range(0, length, CHUNK):
            stream = streams[index, 8 + base : 8 + base + CHUNK]
            running = None
            for shift in range(edge):
                gradient = grads[index, base + shift : base + shift + CHUNK]
                term = taps[index, shift : shift + 1] * gradient
                running = term if running is None else running + term
                tap_sums[shift] = tap_sums[shift] + jnp.sum(
                    (gradient * stream).reshape(CHUNK // 8, 8, LANES), axis=0
                )
            outs[index][base : base + CHUNK] = running.astype(bf16)
        for shift in range(edge):
            grad_short[index, shift : shift + 1] = jnp.sum(tap_sums[shift], axis=0, keepdims=True)


def mixer(gate_in, gate_out, values, cot, taps, medium, group_width):
    length, cols = gate_in.shape
    span, group_count = medium.shape
    edge = taps.shape[1]
    lifted = medium.astype(jnp.float32).T
    zeros = jnp.zeros((group_count, span), jnp.float32)
    ahead = jnp.concatenate([zeros[:, :1], lifted[:, ::-1], zeros[:, 1:]], axis=1)
    behind = jnp.concatenate([lifted, zeros], axis=1)
    groups = LANES // group_width
    rows = pl.BlockSpec((length, LANES), lambda i: (0, i))
    taps_spec = pl.BlockSpec((3, edge, LANES), lambda i: (0, 0, i))
    group_spec = pl.BlockSpec((groups, 2 * span), lambda i: (i, 0))
    f32, bf16 = jnp.float32, jnp.bfloat16
    outs = pl.pallas_call(
        functools.partial(mixer_kernel, group_width),
        grid=(cols // LANES,),
        out_shape=[jax.ShapeDtypeStruct((length, cols), bf16)] * 4
        + [
            jax.ShapeDtypeStruct((3, edge, cols), f32),
            jax.ShapeDtypeStruct((group_count, 2 * span), f32),
        ],
        in_specs=[rows] * 4 + [taps_spec, group_spec, group_spec],
        out_specs=[rows] * 4 + [taps_spec, group_spec],
        scratch_shapes=[
            pltpu.VMEM((3, length + 8, LANES), f32),
            pltpu.VMEM((3, length, LANES), f32),
            pltpu.VMEM((3, length + 8, LANES), f32),
            pltpu.VMEM((length + span, LANES), bf16),
            pltpu.VMEM((length + span, LANES), bf16),
            pltpu.VMEM((groups * span, 2 * span), bf16),
            pltpu.VMEM((groups * span, 2 * span), bf16),
            pltpu.VMEM((length, LANES), f32),
            pltpu.VMEM((length, LANES), f32),
        ],
        compiler_params=pltpu.CompilerParams(vmem_limit_bytes=40 * 2**20),
    )(gate_in, gate_out, values, cot, taps, ahead, behind)
    return (*outs[:5], outs[5][:, 1 : span + 1][:, ::-1].T)


def local(features, gate_in, gate_out, value_weight, short_taps, medium_taps, cotangent):
    ctx = lax.axis_size("ctx")
    dp = lax.axis_size("dp")
    ctx_index = lax.axis_index("ctx")
    rows, channels = features.shape
    cols = value_weight.shape[1]
    span, group_count = medium_taps.shape
    group_width = channels // group_count
    total_rows = rows * ctx * dp
    row_scale = 1.0 / math.sqrt(total_rows)
    group_scale = 1.0 / math.sqrt(total_rows * group_width)
    f32, bf16 = jnp.float32, jnp.bfloat16
    taps = lax.dynamic_slice_in_dim(short_taps, ctx_index * cols, cols, 2)
    own_groups = group_count // ctx
    medium = lax.dynamic_slice_in_dim(medium_taps, ctx_index * own_groups, own_groups, 1)
    window, block_in, block_out, block_cot, weight = gather_all(
        dp, ctx, features, gate_in, gate_out, cotangent, value_weight
    )
    values = jnp.dot(window, weight, preferred_element_type=f32).astype(bf16)
    layer, grad_in, grad_out, grad_values, grad_short, grad_medium = mixer(
        block_in, block_out, values, block_cot, taps, medium, group_width
    )
    grad_weight = (
        lax.dot_general(window, grad_values, (((0,), (0,)), ((), ())), preferred_element_type=f32)
        * row_scale
    ).astype(bf16)
    terms = lax.dot_general(
        grad_values, weight, (((1,), (1,)), ((), ())), preferred_element_type=f32
    ).astype(bf16)
    short_size, medium_size = grad_short.size, grad_medium.size
    flat = jnp.concatenate(
        [(grad_short * row_scale).reshape(-1), (grad_medium * group_scale).reshape(-1)]
    )
    pad = -flat.size % (16 * cols)
    small = jnp.pad(flat, (0, pad)).astype(bf16).reshape(-1, cols)
    weight_out, terms_out, layer_out, first_out, second_out, small_out = scatter_all(
        dp, ctx, grad_weight, terms, layer, grad_in, grad_out, small
    )
    grad_features = jnp.sum(terms_out.astype(f32), axis=0).astype(bf16)
    sums = jnp.sum(small_out.astype(f32), axis=0).reshape(-1)
    return (
        layer_out,
        grad_features,
        first_out,
        second_out,
        weight_out,
        sums[:short_size].reshape(grad_short.shape),
        sums[short_size : short_size + medium_size].reshape(grad_medium.shape),
    )


def solution(mesh):
    rows, split = P(("dp", "ctx"), None), P("dp", "ctx")
    return jax.shard_map(
        local,
        mesh=mesh,
        in_specs=(rows, rows, rows, split, P(), P(), rows),
        out_specs=(rows, rows, rows, rows, split, P(None, None, "ctx"), P(None, "ctx")),
        check_vma=False,
    )
```

```python
import functools
import math

import jax
import jax.numpy as jnp
from jax import lax
from jax.experimental import pallas as pl
from jax.experimental.pallas import tpu as pltpu
from jax.sharding import PartitionSpec as P

MESH = pl.DeviceIdType.MESH
ANY = pl.BlockSpec(memory_space=pl.ANY)
LANES = 128
CHUNK = 64
VMEM = pl.BlockSpec(memory_space=pltpu.VMEM)
F32, BF16 = jnp.float32, jnp.bfloat16


def greet(dp, ctx):
    me_dp, me_ctx = lax.axis_index("dp"), lax.axis_index("ctx")
    barrier = pltpu.get_barrier_semaphore()
    for step in range(1, dp):
        pl.semaphore_signal(
            barrier, inc=1, device_id=(lax.rem(me_dp + step, dp), me_ctx), device_id_type=MESH
        )
    for step in range(1, ctx):
        pl.semaphore_signal(
            barrier, inc=1, device_id=(me_dp, lax.rem(me_ctx + step, ctx)), device_id_type=MESH
        )
    pl.semaphore_wait(barrier, dp + ctx - 2)


def send(src, dst, send_sem, recv_sem, device):
    return pltpu.make_async_remote_copy(
        src_ref=src,
        dst_ref=dst,
        send_sem=send_sem,
        recv_sem=recv_sem,
        device_id=device,
        device_id_type=MESH,
    )


def spread(source, target, groups, span):
    offset = lax.broadcasted_iota(jnp.int32, (8, 2 * span), 0)
    for group in range(groups):
        rows = jnp.broadcast_to(source[group : group + 1], (8, 2 * span))
        for bit in (1, 2, 4):
            rows = jnp.where((offset & bit) != 0, pltpu.roll(rows, bit, 1), rows)
        height = 8
        while height < span:
            rows = jnp.concatenate([rows, pltpu.roll(rows, height, 1)], axis=0)
            height *= 2
        target[group * span : (group + 1) * span] = rows.astype(BF16)


def filter_back(table, source, target, length, groups, span, owner):
    for base in range(0, length, span):
        chosen = None
        for group in range(groups):
            out = jnp.dot(
                table[group * span : (group + 1) * span], source[base : base + 2 * span],
                preferred_element_type=F32,
            )
            chosen = out if chosen is None else jnp.where(owner == group, out, chosen)
        target[base : base + span] = chosen


def ahead_conv(taps, index, stream, base, edge):
    running = taps[index, 0:1] * stream[8 + base : 8 + base + CHUNK]
    for shift in range(1, edge):
        start = 8 + base - shift
        running = running + taps[index, shift : shift + 1] * stream[start : start + CHUNK]
    return running


def clear(scratch, length, span):
    streams, _, grads, product, grad_filtered = scratch[:5]
    streams[:, :8] = jnp.zeros((3, 8, LANES), F32)
    grads[:, length:] = jnp.zeros((3, 8, LANES), F32)
    product[:span] = jnp.zeros((span, LANES), BF16)
    grad_filtered[length:] = jnp.zeros((span, LANES), BF16)


def values_gradient(group_width, gate_in, gate_out, cot, taps, behind, grad_values, scratch):
    streams, convs, grads, _, grad_filtered, _, back, _, grad_product = scratch
    length, edge, span = gate_in.shape[0], taps.shape[1], back.shape[1] // 2
    groups = LANES // group_width
    streams[0, 8:] = gate_in[...].astype(F32)
    streams[1, 8:] = gate_out[...].astype(F32)
    spread(behind, back, groups, span)
    for base in range(0, length, CHUNK):
        part = slice(base, base + CHUNK)
        convs[0, part] = ahead_conv(taps, 0, streams.at[0], base, edge)
        conv = ahead_conv(taps, 1, streams.at[1], base, edge)
        grad_filtered[part] = (cot[part].astype(F32) * conv).astype(BF16)
    owner = lax.broadcasted_iota(jnp.int32, (span, LANES), 1) // group_width
    filter_back(back, grad_filtered, grad_product, length, groups, span, owner)
    grads[2, :length] = grad_product[...] * convs[0]
    for base in range(0, length, CHUNK):
        running = taps[2, 0:1] * grads[2, base : base + CHUNK]
        for shift in range(1, edge):
            start = base + shift
            running = running + taps[2, shift : shift + 1] * grads[2, start : start + CHUNK]
        grad_values[base : base + CHUNK] = running.astype(BF16)


def mixer_block(
    group_width, gate_in, gate_out, values, cot, taps, ahead, behind,
    layer, grad_in, grad_out, grad_short, grad_medium, scratch,
):
    streams, convs, grads, product, grad_filtered, table, back, filtered, grad_product = scratch
    length, edge, span = gate_in.shape[0], taps.shape[1], back.shape[1] // 2
    groups = LANES // group_width
    for index, stream in enumerate((gate_in, gate_out, values)):
        streams[index, 8:] = stream[...].astype(F32)
    spread(ahead, table, groups, span)
    spread(behind, back, groups, span)
    for base in range(0, length, CHUNK):
        part = slice(base, base + CHUNK)
        conv = [ahead_conv(taps, index, streams.at[index], base, edge) for index in range(3)]
        for index in range(3):
            convs[index, part] = conv[index]
        product[span + base : span + base + CHUNK] = (conv[0] * conv[2]).astype(BF16)
        grad_filtered[part] = (cot[part].astype(F32) * conv[1]).astype(BF16)
    owner = lax.broadcasted_iota(jnp.int32, (span, LANES), 1) // group_width
    filter_back(table, product, filtered, length, groups, span, owner)
    filter_back(back, grad_filtered, grad_product, length, groups, span, owner)
    offset = lax.broadcasted_iota(jnp.int32, (8, 2 * span), 0)
    for group in range(groups):
        total = None
        for base in range(0, length, span):
            current = grad_filtered[base : base + span].astype(F32)
            current = jnp.where(owner == group, current, 0.0).astype(BF16)
            term = lax.dot_general(
                current, product[base : base + 2 * span], (((1,), (1,)), ((), ())),
                preferred_element_type=F32,
            )
            total = term if total is None else total + term
        height = span // 2
        while height >= 8:
            total = total[:height] + pltpu.roll(total[height:], 2 * span - height, 1)
            height //= 2
        for bit in (1, 2, 4):
            total = jnp.where((offset & bit) != 0, pltpu.roll(total, 2 * span - bit, 1), total)
        total = pltpu.roll(total, 2 * span - 1, 1)
        grad_medium[group : group + 1] = jnp.sum(total, axis=0, keepdims=True)[:, :span]
    for base in range(0, length, CHUNK):
        part = slice(base, base + CHUNK)
        kept = filtered[part]
        gradient = grad_product[part]
        layer[part] = (convs[1, part] * kept).astype(BF16)
        grads[0, part] = gradient * convs[2, part]
        grads[1, part] = cot[part].astype(F32) * kept
        grads[2, part] = gradient * convs[0, part]
    outs = (grad_in, grad_out, None)
    for index in range(3):
        tap_sums = [jnp.zeros((8, LANES), F32) for _ in range(edge)]
        for base in range(0, length, CHUNK):
            stream = streams[index, 8 + base : 8 + base + CHUNK]
            running = None
            for shift in range(edge):
                gradient = grads[index, base + shift : base + shift + CHUNK]
                if index < 2:
                    term = taps[index, shift : shift + 1] * gradient
                    running = term if running is None else running + term
                tap_sums[shift] = tap_sums[shift] + jnp.sum(
                    (gradient * stream).reshape(CHUNK // 8, 8, LANES), axis=0
                )
            if index < 2:
                outs[index][base : base + CHUNK] = running.astype(BF16)
        for shift in range(edge):
            grad_short[8 * index + shift : 8 * index + shift + 1] = jnp.sum(
                tap_sums[shift], axis=0, keepdims=True
            )


def mixer_scratch(length, span, group_width):
    groups = LANES // group_width
    f32, bf16 = (lambda *shape: pltpu.VMEM(shape, F32)), (lambda *shape: pltpu.VMEM(shape, BF16))
    return [
        f32(3, length + 8, LANES), f32(3, length, LANES), f32(3, length + 8, LANES),
        bf16(length + span, LANES), bf16(length + span, LANES),
        bf16(groups * span, 2 * span), bf16(groups * span, 2 * span),
        f32(length, LANES), f32(length, LANES),
    ]


def lane_block(step):
    return pl.ds(pl.multiple_of(step * LANES, LANES), LANES)


def group_rows(step, groups):
    return pl.ds(pl.multiple_of(step * groups, groups), groups)


def gather_kernel(
    dp, ctx, pair,
    group_width,
    features, gate_in, gate_out, cot, weight, taps, behind,
    window_out, in_out, out_out, cot_out, values, grad_values, terms,
    window, block_in, block_out, block_cot, full, total,
    local_sem, ctx_send, ctx_recv, right_send, left_send, pair_send, full_recv, out_sem,
    *scratch,
):
    me_dp, me_ctx = lax.axis_index("dp"), lax.axis_index("ctx")
    line = dp // pair
    at, side = me_dp // pair, lax.rem(me_dp, pair)
    rows = features.shape[0]
    cols, depth = weight.shape[1], weight.shape[0]
    greet(dp, ctx)

    def block(index):
        return full.at[index]

    def push(src, index, sem, to):
        return send(src, block(index), sem, full_recv.at[index], (to, me_ctx))

    def others(index, src):
        if pair == 2:
            push(src, index, pair_send.at[index // pair], at * pair + 1 - side).start()

    @pl.when(at + 1 < line)
    def _():
        push(weight, me_dp, right_send.at[at], me_dp + pair).start()

    @pl.when(at > 0)
    def _():
        push(weight, me_dp, left_send.at[at], me_dp - pair).start()

    others(me_dp, weight)

    mine = pl.ds(pl.multiple_of(me_ctx * rows, rows), rows)
    streams = ((gate_in, block_in), (gate_out, block_out), (cot, block_cot))
    copies = {}
    for which, (src, dst) in enumerate(((features, window),) + streams):
        copies[which] = []
        for step in range(1, ctx):
            peer = lax.rem(me_ctx + step, ctx)
            part = src if which == 0 else src.at[:, pl.ds(pl.multiple_of(peer * cols, cols), cols)]
            copies[which].append(
                send(
                    part, dst.at[mine], ctx_send.at[which, step], ctx_recv.at[which, step],
                    (me_dp, peer),
                )
            )
    for which in (1, 2, 3):
        for copy in copies[which]:
            copy.start()
    stays = [pltpu.make_async_copy(weight, block(me_dp), local_sem.at[4])]
    stays.append(pltpu.make_async_copy(features, window.at[mine], local_sem.at[0]))
    for which, (src, dst) in enumerate(streams):
        part = src.at[:, pl.ds(pl.multiple_of(me_ctx * cols, cols), cols)]
        stays.append(pltpu.make_async_copy(part, dst.at[mine], local_sem.at[which + 1]))
    for copy in stays:
        copy.start()

    def arrived(index):
        push(block(index), index, right_send.at[0], me_dp).wait_recv()

    def relay(far):
        @pl.when(at - far >= 0)
        def _():
            index = me_dp - far * pair
            arrived(index)

            @pl.when(at + 1 < line)
            def _():
                push(block(index), index, right_send.at[at - far], me_dp + pair).start()

            others(index, block(index))

        @pl.when(at + far < line)
        def _():
            index = me_dp + far * pair
            arrived(index)

            @pl.when(at > 0)
            def _():
                push(block(index), index, left_send.at[at + far], me_dp - pair).start()

            others(index, block(index))

    steps = cols // LANES
    groups = LANES // group_width
    length = window.shape[0]
    clear(scratch, length, scratch[6].shape[1] // 2)

    def gradient_step(step, carry):
        lanes = lane_block(step)
        values_gradient(
            group_width, block_in.at[:, lanes], block_out.at[:, lanes], block_cot.at[:, lanes],
            taps.at[:, :, lanes], behind.at[group_rows(step, groups)], grad_values.at[:, lanes],
            scratch,
        )
        return carry

    def add_terms(index):
        part = pl.ds(pl.multiple_of(index * depth, depth), depth)
        terms[:, part] = lax.dot_general(
            grad_values[...], full[index], (((1,), (1,)), ((), ())), preferred_element_type=F32
        ).astype(BF16)

    def add_values(index):
        part = pl.ds(pl.multiple_of(index * depth, depth), depth)
        total[...] += jnp.dot(window[:, part], full[index], preferred_element_type=F32)

    if line > 1:
        relay(1)
    for which in (1, 2, 3):
        for copy in copies[which]:
            copy.wait()
    for copy in copies[0]:
        copy.start()
    for copy in stays:
        copy.wait()
    leaves = [
        pltpu.make_async_copy(src, dst, out_sem.at[which])
        for which, (src, dst) in enumerate(
            ((block_in, in_out), (block_out, out_out), (block_cot, cot_out), (window, window_out))
        )
    ]
    for leave in leaves[:3]:
        leave.start()
    total[...] = jnp.zeros_like(total)
    lax.fori_loop(0, steps // 2, gradient_step, 0)
    if line > 2:
        relay(2)
    lax.fori_loop(steps // 2, steps, gradient_step, 0)
    for far in range(3, line):
        relay(far)

    def near_terms(spot, carry):
        add_terms(spot * pair + side)
        return carry

    def near_values(spot, carry):
        add_values(spot * pair + side)
        return carry

    def far_both(step, carry):
        index = lax.rem(at + step, line) * pair + 1 - side
        arrived(index)
        add_terms(index)
        add_values(index)
        return carry

    lax.fori_loop(0, line, near_terms, 0)
    for copy in copies[0]:
        copy.wait()
    leaves[3].start()
    lax.fori_loop(0, line, near_values, 0)
    if pair == 2:
        lax.fori_loop(0, line, far_both, 0)
    values[...] = total[...].astype(BF16)
    for leave in leaves:
        leave.wait()
    for spot in range(line):
        if pair == 2:
            push(weight, me_dp, pair_send.at[spot], me_dp).wait_send()

        @pl.when((at + 1 < line) & (spot <= at))
        def _():
            push(weight, me_dp, right_send.at[spot], me_dp).wait_send()

        @pl.when((at > 0) & (spot >= at))
        def _():
            push(weight, me_dp, left_send.at[spot], me_dp).wait_send()


def gather_all(dp, ctx, group_width, features, gate_in, gate_out, cot, weight, taps, behind):
    pair = 2 if dp % 2 == 0 else 1
    rows, channels = features.shape
    depth, cols = weight.shape
    length = rows * ctx
    span = behind.shape[1] // 2
    shapes = [(length, channels)] + [(length, cols)] * 5 + [(length, channels)]
    dma = pltpu.SemaphoreType.DMA
    line = dp // pair
    block = pltpu.VMEM((length, cols), BF16)
    return pl.pallas_call(
        functools.partial(gather_kernel, dp, ctx, pair, group_width),
        out_shape=[jax.ShapeDtypeStruct(shape, BF16) for shape in shapes],
        in_specs=[ANY] * 5 + [VMEM] * 2,
        out_specs=[ANY] * 4 + [VMEM] * 3,
        scratch_shapes=[
            pltpu.VMEM((length, channels), BF16), block, block, block,
            pltpu.VMEM((dp, depth, cols), BF16), pltpu.VMEM((length, cols), F32),
            dma((5,)), dma((4, ctx)), dma((4, ctx)), dma((line,)), dma((line,)), dma((line,)),
            dma((dp,)), dma((4,)),
        ]
        + mixer_scratch(length, span, group_width),
        compiler_params=pltpu.CompilerParams(
            collective_id=0, has_side_effects=True, vmem_limit_bytes=50 * 2**20
        ),
    )(features, gate_in, gate_out, cot, weight, taps, behind)


def scatter_kernel(
    dp, ctx, pair,
    group_width, row_scale, group_scale,
    grad_weight, terms, gate_in, gate_out, values, cot, taps, ahead, behind,
    weight_out, features_out, layer_out, first_out, second_out, short_out, medium_out,
    held, from_pair, from_left, from_right,
    terms_in, layer, first, second, short, medium, short_send, medium_send, short_in, medium_in,
    local_sem, held_sem, ctx_send, ctx_recv, small_send, small_recv,
    pair_send, pair_recv, right_send, left_recv, left_send, right_recv, out_sem,
    *scratch,
):
    me_dp, me_ctx = lax.axis_index("dp"), lax.axis_index("ctx")
    line = dp // pair
    at, side = me_dp // pair, lax.rem(me_dp, pair)
    rows, cols = layer_out.shape[0], layer.shape[1]
    depth = weight_out.shape[0]
    greet(dp, ctx)

    def block(index):
        return grad_weight.at[pl.ds(pl.multiple_of(index * depth, depth), depth)]

    def keep(spot):
        return pltpu.make_async_copy(block(spot * pair + side), held.at[spot], held_sem.at[spot])

    def swap(spot):
        return send(
            block(spot * pair + 1 - side), from_pair.at[spot], pair_send.at[spot],
            pair_recv.at[spot], (at * pair + 1 - side, me_ctx),
        )

    def to_right(spot):
        return send(
            held.at[spot], from_left.at[spot], right_send.at[spot], left_recv.at[spot],
            (me_dp + pair, me_ctx),
        )

    def to_left(spot):
        return send(
            held.at[spot], from_right.at[spot], left_send.at[spot], right_recv.at[spot],
            (me_dp - pair, me_ctx),
        )

    def begin(spot):
        if pair == 2:
            swap(spot).start()
        keep(spot).start()

    for far in range(line - 1, 0, -1):
        pl.when(at + far < line)(functools.partial(begin, at + far))
        pl.when(at - far >= 0)(functools.partial(begin, at - far))
    begin(at)

    copies = {}
    mine = pl.ds(pl.multiple_of(me_ctx * cols, cols), cols)
    outs = ((layer, layer_out), (first, first_out), (second, second_out))
    for which, (src, dst) in enumerate(((terms, terms_in),) + outs):
        group = copies.setdefault(which, [])
        for step in range(1, ctx):
            peer = lax.rem(me_ctx + step, ctx)
            group.append(
                send(
                    src.at[pl.ds(pl.multiple_of(peer * rows, rows), rows)],
                    dst.at[me_ctx] if which == 0 else dst.at[:, mine],
                    ctx_send.at[which, step], ctx_recv.at[which, step], (me_dp, peer),
                )
            )
        part = src.at[pl.ds(pl.multiple_of(me_ctx * rows, rows), rows)]
        group.append(
            pltpu.make_async_copy(
                part, dst.at[me_ctx] if which == 0 else dst.at[:, mine], local_sem.at[which]
            )
        )
    group = copies.setdefault(4, [])
    for kind, (src, dst) in enumerate(((short_send, short_in), (medium_send, medium_in))):
        for step in range(1, dp):
            peer = lax.rem(me_dp + step, dp)
            group.append(
                send(
                    src, dst.at[me_dp], small_send.at[kind, step], small_recv.at[kind, step],
                    (peer, me_ctx),
                )
            )
        group.append(pltpu.make_async_copy(src, dst.at[me_dp], local_sem.at[4 + kind]))
    for copy in copies[0]:
        copy.start()

    steps = layer.shape[1] // LANES
    groups = LANES // group_width
    clear(scratch, layer.shape[0], scratch[6].shape[1] // 2)
    short[...] = jnp.zeros_like(short)

    def mixer_step(step, carry):
        lanes, owned = lane_block(step), group_rows(step, groups)
        mixer_block(
            group_width, gate_in.at[:, lanes], gate_out.at[:, lanes], values.at[:, lanes],
            cot.at[:, lanes], taps.at[:, :, lanes], ahead.at[owned], behind.at[owned],
            layer.at[:, lanes], first.at[:, lanes], second.at[:, lanes], short.at[:, lanes],
            medium.at[owned], scratch,
        )
        return carry

    span = 32

    def add(spot, source):
        def body(step, carry):
            part = pl.ds(pl.multiple_of(step * span, span), span)
            held[spot, part] = (
                held[spot, part].astype(jnp.float32) + source[spot, part].astype(jnp.float32)
            ).astype(jnp.bfloat16)
            return carry

        lax.fori_loop(0, depth // span, body, 0)

    def ready(spot):
        keep(spot).wait()
        if pair == 2:
            swap(spot).wait_recv()
            add(spot, from_pair)

    def go_right(spot):
        ready(spot)

        @pl.when(at > 0)
        def _():
            to_right(spot).wait_recv()
            add(spot, from_left)

        to_right(spot).start()

    def go_left(spot):
        ready(spot)

        @pl.when(at + 1 < line)
        def _():
            to_left(spot).wait_recv()
            add(spot, from_right)

        to_left(spot).start()

    early = steps * 5 // 8
    lax.fori_loop(0, early, mixer_step, 0)
    for far in range(line - 1, 0, -1):
        pl.when(at + far < line)(functools.partial(go_right, at + far))
        pl.when(at - far >= 0)(functools.partial(go_left, at - far))
        if far == line - 1:
            lax.fori_loop(early, steps, mixer_step, 0)
            short_send[...] = (short[...] * row_scale).astype(BF16)
            medium_send[...] = (medium[...] * group_scale).astype(BF16)
            for which in (1, 2, 3, 4):
                for copy in copies[which]:
                    copy.start()
    for copy in copies[0]:
        copy.wait()

    def sum_terms(step, carry):
        part = pl.ds(pl.multiple_of(step * 16, 16), 16)
        summed = terms_in[0, part].astype(F32)
        for peer in range(1, ctx):
            summed = summed + terms_in[peer, part].astype(F32)
        features_out[part] = summed.astype(BF16)
        return carry

    lax.fori_loop(0, rows // 16, sum_terms, 0)
    for copy in copies[4]:
        copy.wait()
    summed = short_in[0].astype(F32)
    whole = medium_in[0].astype(F32)
    for peer in range(1, dp):
        summed = summed + short_in[peer].astype(F32)
        whole = whole + medium_in[peer].astype(F32)
    edge = short_out.shape[1]
    for index in range(3):
        short_out[index] = summed[8 * index : 8 * index + edge]
    medium_out[...] = whole
    ready(at)

    @pl.when(at > 0)
    def _():
        to_right(at).wait_recv()
        add(at, from_left)

    @pl.when(at + 1 < line)
    def _():
        to_left(at).wait_recv()
        add(at, from_right)

    result = pltpu.make_async_copy(held.at[at], weight_out, out_sem)
    result.start()
    for which in (1, 2, 3):
        for copy in copies[which]:
            copy.wait()
    for spot in range(line):
        if pair == 2:
            swap(spot).wait_send()
        pl.when(spot > at)(lambda spot=spot: to_right(spot).wait_send())
        pl.when(spot < at)(lambda spot=spot: to_left(spot).wait_send())
    result.wait()


def scatter_all(
    dp, ctx, group_width, row_scale, group_scale,
    grad_weight, terms, gate_in, gate_out, values, cot, taps, ahead, behind,
):
    pair = 2 if dp % 2 == 0 else 1
    line = dp // pair
    length, cols = values.shape
    edge, span = taps.shape[1], ahead.shape[1] // 2
    group_count = ahead.shape[0]
    rows, channels, depth = length // ctx, terms.shape[1], grad_weight.shape[0] // dp
    shapes = [(depth, cols)] + [(rows, channels)] * 4
    dma = pltpu.SemaphoreType.DMA
    slots = pltpu.VMEM((line, depth, cols), BF16)
    block = pltpu.VMEM((length, cols), BF16)
    return pl.pallas_call(
        functools.partial(scatter_kernel, dp, ctx, pair, group_width, row_scale, group_scale),
        out_shape=[jax.ShapeDtypeStruct(shape, BF16) for shape in shapes]
        + [
            jax.ShapeDtypeStruct((3, edge, cols), F32),
            jax.ShapeDtypeStruct((group_count, span), F32),
        ],
        in_specs=[ANY] * 2 + [VMEM] * 7,
        out_specs=[ANY, VMEM] + [ANY] * 3 + [VMEM] * 2,
        scratch_shapes=[slots] * 4
        + [
            pltpu.VMEM((ctx, rows, channels), BF16), block, block, block,
            pltpu.VMEM((32, cols), F32), pltpu.VMEM((group_count, span), F32),
            pltpu.VMEM((32, cols), BF16), pltpu.VMEM((group_count, span), BF16),
            pltpu.VMEM((dp, 32, cols), BF16), pltpu.VMEM((dp, group_count, span), BF16),
        ]
        + [dma((6,)), dma((line,)), dma((4, ctx)), dma((4, ctx)), dma((2, dp)), dma((2, dp))]
        + [dma((line,))] * 6
        + [dma]
        + mixer_scratch(length, span, group_width),
        compiler_params=pltpu.CompilerParams(
            collective_id=1, has_side_effects=True, vmem_limit_bytes=50 * 2**20
        ),
    )(grad_weight, terms, gate_in, gate_out, values, cot, taps, ahead, behind)


def local(features, gate_in, gate_out, value_weight, short_taps, medium_taps, cotangent):
    ctx = lax.axis_size("ctx")
    dp = lax.axis_size("dp")
    ctx_index = lax.axis_index("ctx")
    rows, channels = features.shape
    cols = value_weight.shape[1]
    span, group_count = medium_taps.shape
    group_width = channels // group_count
    total_rows = rows * ctx * dp
    row_scale = 1.0 / math.sqrt(total_rows)
    group_scale = 1.0 / math.sqrt(total_rows * group_width)
    taps = lax.dynamic_slice_in_dim(short_taps, ctx_index * cols, cols, 2)
    own_groups = group_count // ctx
    medium = lax.dynamic_slice_in_dim(medium_taps, ctx_index * own_groups, own_groups, 1)
    lifted = medium.astype(F32).T
    zeros = jnp.zeros((own_groups, span), F32)
    ahead = jnp.concatenate([zeros[:, :1], lifted[:, ::-1], zeros[:, 1:]], axis=1)
    behind = jnp.concatenate([lifted, zeros], axis=1)
    window, block_in, block_out, block_cot, values, grad_values, terms = gather_all(
        dp, ctx, group_width, features, gate_in, gate_out, cotangent, value_weight, taps, behind
    )
    grad_weight = (
        lax.dot_general(window, grad_values, (((0,), (0,)), ((), ())), preferred_element_type=F32)
        * row_scale
    ).astype(BF16)
    weight_out, grad_features, layer_out, first_out, second_out, grad_short, grad_medium = (
        scatter_all(
            dp, ctx, group_width, row_scale, group_scale,
            grad_weight, terms, block_in, block_out, values, block_cot, taps, ahead, behind,
        )
    )
    return (
        layer_out,
        grad_features,
        first_out,
        second_out,
        weight_out,
        grad_short,
        grad_medium[:, ::-1].T,
    )


def solution(mesh):
    rows, split = P(("dp", "ctx"), None), P("dp", "ctx")
    return jax.shard_map(
        local,
        mesh=mesh,
        in_specs=(rows, rows, rows, split, P(), P(), rows),
        out_specs=(rows, rows, rows, rows, split, P(None, None, "ctx"), P(None, "ctx")),
        check_vma=False,
    )
```

```python
import functools
import math

import jax
import jax.numpy as jnp
from jax import lax
from jax.experimental import pallas as pl
from jax.experimental.pallas import tpu as pltpu
from jax.sharding import PartitionSpec as P

MESH = pl.DeviceIdType.MESH
ANY = pl.BlockSpec(memory_space=pl.ANY)
LANES = 128
CHUNK = 64
VMEM = pl.BlockSpec(memory_space=pltpu.VMEM)
F32, BF16 = jnp.float32, jnp.bfloat16


def greet(dp, ctx):
    me_dp, me_ctx = lax.axis_index("dp"), lax.axis_index("ctx")
    barrier = pltpu.get_barrier_semaphore()
    for step in range(1, dp):
        pl.semaphore_signal(
            barrier, inc=1, device_id=(lax.rem(me_dp + step, dp), me_ctx), device_id_type=MESH
        )
    for step in range(1, ctx):
        pl.semaphore_signal(
            barrier, inc=1, device_id=(me_dp, lax.rem(me_ctx + step, ctx)), device_id_type=MESH
        )
    pl.semaphore_wait(barrier, dp + ctx - 2)


def send(src, dst, send_sem, recv_sem, device):
    return pltpu.make_async_remote_copy(
        src_ref=src,
        dst_ref=dst,
        send_sem=send_sem,
        recv_sem=recv_sem,
        device_id=device,
        device_id_type=MESH,
    )


def spread(source, target, groups, span):
    offset = lax.broadcasted_iota(jnp.int32, (8, 2 * span), 0)
    for group in range(groups):
        rows = jnp.broadcast_to(source[group : group + 1], (8, 2 * span))
        for bit in (1, 2, 4):
            rows = jnp.where((offset & bit) != 0, pltpu.roll(rows, bit, 1), rows)
        height = 8
        while height < span:
            rows = jnp.concatenate([rows, pltpu.roll(rows, height, 1)], axis=0)
            height *= 2
        target[group * span : (group + 1) * span] = rows.astype(BF16)


def filter_back(table, source, target, length, groups, span, owner):
    for base in range(0, length, span):
        chosen = None
        for group in range(groups):
            out = jnp.dot(
                table[group * span : (group + 1) * span], source[base : base + 2 * span],
                preferred_element_type=F32,
            )
            chosen = out if chosen is None else jnp.where(owner == group, out, chosen)
        target[base : base + span] = chosen


def ahead_conv(taps, index, stream, base, edge):
    running = taps[index, 0:1] * stream[8 + base : 8 + base + CHUNK]
    for shift in range(1, edge):
        start = 8 + base - shift
        running = running + taps[index, shift : shift + 1] * stream[start : start + CHUNK]
    return running


def clear(scratch, length, span):
    streams, _, grads, product, grad_filtered = scratch[:5]
    streams[:, :8] = jnp.zeros((3, 8, LANES), F32)
    grads[:, length:] = jnp.zeros((3, 8, LANES), F32)
    product[:span] = jnp.zeros((span, LANES), BF16)
    grad_filtered[length:] = jnp.zeros((span, LANES), BF16)


def values_gradient(group_width, gate_in, gate_out, cot, taps, behind, grad_values, scratch):
    streams, convs, grads, _, grad_filtered, _, back, _, grad_product = scratch
    length, edge, span = gate_in.shape[0], taps.shape[1], back.shape[1] // 2
    groups = LANES // group_width
    streams[0, 8:] = gate_in[...].astype(F32)
    streams[1, 8:] = gate_out[...].astype(F32)
    spread(behind, back, groups, span)
    for base in range(0, length, CHUNK):
        part = slice(base, base + CHUNK)
        convs[0, part] = ahead_conv(taps, 0, streams.at[0], base, edge)
        conv = ahead_conv(taps, 1, streams.at[1], base, edge)
        grad_filtered[part] = (cot[part].astype(F32) * conv).astype(BF16)
    owner = lax.broadcasted_iota(jnp.int32, (span, LANES), 1) // group_width
    filter_back(back, grad_filtered, grad_product, length, groups, span, owner)
    grads[2, :length] = grad_product[...] * convs[0]
    for base in range(0, length, CHUNK):
        running = taps[2, 0:1] * grads[2, base : base + CHUNK]
        for shift in range(1, edge):
            start = base + shift
            running = running + taps[2, shift : shift + 1] * grads[2, start : start + CHUNK]
        grad_values[base : base + CHUNK] = running.astype(BF16)


def mixer_block(
    group_width, gate_in, gate_out, values, cot, taps, ahead, behind,
    layer, grad_in, grad_out, grad_short, grad_medium, scratch,
):
    streams, convs, grads, product, grad_filtered, table, back, filtered, grad_product = scratch
    length, edge, span = gate_in.shape[0], taps.shape[1], back.shape[1] // 2
    groups = LANES // group_width
    for index, stream in enumerate((gate_in, gate_out, values)):
        streams[index, 8:] = stream[...].astype(F32)
    spread(ahead, table, groups, span)
    spread(behind, back, groups, span)
    for base in range(0, length, CHUNK):
        part = slice(base, base + CHUNK)
        conv = [ahead_conv(taps, index, streams.at[index], base, edge) for index in range(3)]
        for index in range(3):
            convs[index, part] = conv[index]
        product[span + base : span + base + CHUNK] = (conv[0] * conv[2]).astype(BF16)
        grad_filtered[part] = (cot[part].astype(F32) * conv[1]).astype(BF16)
    owner = lax.broadcasted_iota(jnp.int32, (span, LANES), 1) // group_width
    filter_back(table, product, filtered, length, groups, span, owner)
    filter_back(back, grad_filtered, grad_product, length, groups, span, owner)
    offset = lax.broadcasted_iota(jnp.int32, (8, 2 * span), 0)
    for group in range(groups):
        total = None
        for base in range(0, length, span):
            current = grad_filtered[base : base + span].astype(F32)
            current = jnp.where(owner == group, current, 0.0).astype(BF16)
            term = lax.dot_general(
                current, product[base : base + 2 * span], (((1,), (1,)), ((), ())),
                preferred_element_type=F32,
            )
            total = term if total is None else total + term
        height = span // 2
        while height >= 8:
            total = total[:height] + pltpu.roll(total[height:], 2 * span - height, 1)
            height //= 2
        for bit in (1, 2, 4):
            total = jnp.where((offset & bit) != 0, pltpu.roll(total, 2 * span - bit, 1), total)
        total = pltpu.roll(total, 2 * span - 1, 1)
        grad_medium[group : group + 1] = jnp.sum(total, axis=0, keepdims=True)[:, :span]
    for base in range(0, length, CHUNK):
        part = slice(base, base + CHUNK)
        kept = filtered[part]
        gradient = grad_product[part]
        layer[part] = (convs[1, part] * kept).astype(BF16)
        grads[0, part] = gradient * convs[2, part]
        grads[1, part] = cot[part].astype(F32) * kept
        grads[2, part] = gradient * convs[0, part]
    outs = (grad_in, grad_out, None)
    for index in range(3):
        tap_sums = [jnp.zeros((8, LANES), F32) for _ in range(edge)]
        for base in range(0, length, CHUNK):
            stream = streams[index, 8 + base : 8 + base + CHUNK]
            running = None
            for shift in range(edge):
                gradient = grads[index, base + shift : base + shift + CHUNK]
                if index < 2:
                    term = taps[index, shift : shift + 1] * gradient
                    running = term if running is None else running + term
                tap_sums[shift] = tap_sums[shift] + jnp.sum(
                    (gradient * stream).reshape(CHUNK // 8, 8, LANES), axis=0
                )
            if index < 2:
                outs[index][base : base + CHUNK] = running.astype(BF16)
        for shift in range(edge):
            grad_short[8 * index + shift : 8 * index + shift + 1] = jnp.sum(
                tap_sums[shift], axis=0, keepdims=True
            )


def mixer_scratch(length, span, group_width):
    groups = LANES // group_width
    f32, bf16 = (lambda *shape: pltpu.VMEM(shape, F32)), (lambda *shape: pltpu.VMEM(shape, BF16))
    return [
        f32(3, length + 8, LANES), f32(3, length, LANES), f32(3, length + 8, LANES),
        bf16(length + span, LANES), bf16(length + span, LANES),
        bf16(groups * span, 2 * span), bf16(groups * span, 2 * span),
        f32(length, LANES), f32(length, LANES),
    ]


def lane_block(step):
    return pl.ds(pl.multiple_of(step * LANES, LANES), LANES)


def group_rows(step, groups):
    return pl.ds(pl.multiple_of(step * groups, groups), groups)


def gather_kernel(
    dp, ctx, pair,
    group_width,
    features, gate_in, gate_out, cot, weight, taps, behind,
    window_out, in_out, out_out, cot_out, values, grad_values, terms,
    window, block_in, block_out, block_cot, full, total,
    local_sem, ctx_send, ctx_recv, right_send, left_send, pair_send, full_recv, out_sem,
    half_send, half_recv,
    *scratch,
):
    me_dp, me_ctx = lax.axis_index("dp"), lax.axis_index("ctx")
    line = dp // pair
    at, side = me_dp // pair, lax.rem(me_dp, pair)
    rows = features.shape[0]
    cols, depth = weight.shape[1], weight.shape[0]
    greet(dp, ctx)

    def block(index):
        return full.at[index]

    def push(src, index, sem, to):
        return send(src, block(index), sem, full_recv.at[index], (to, me_ctx))

    halves = pair == 2 and line % 2 == 0
    buddy = at + 1 - 2 * lax.rem(at, 2)
    half = depth // 2

    def across(index, src):
        return push(src, index, pair_send.at[index // pair], at * pair + 1 - side)

    def across_half(index):
        top = full.at[index, pl.ds(0, half)]
        return send(
            top, top, pair_send.at[index // pair], full_recv.at[index],
            (at * pair + 1 - side, me_ctx),
        )

    def along_half():
        low = full.at[at * pair + 1 - side, pl.ds(half, half)]
        return send(low, low, half_send, half_recv, (buddy * pair + side, me_ctx))

    def others(index, src):
        if halves:
            pl.when(index // pair == buddy)(lambda: across_half(index).start())
            pl.when(index // pair != buddy)(lambda: across(index, src).start())
        elif pair == 2:
            across(index, src).start()

    @pl.when(at + 1 < line)
    def _():
        push(weight, me_dp, right_send.at[at], me_dp + pair).start()

    @pl.when(at > 0)
    def _():
        push(weight, me_dp, left_send.at[at], me_dp - pair).start()

    others(me_dp, weight)

    mine = pl.ds(pl.multiple_of(me_ctx * rows, rows), rows)
    streams = ((gate_in, block_in), (gate_out, block_out), (cot, block_cot))
    copies = {}
    for which, (src, dst) in enumerate(((features, window),) + streams):
        copies[which] = []
        for step in range(1, ctx):
            peer = lax.rem(me_ctx + step, ctx)
            part = src if which == 0 else src.at[:, pl.ds(pl.multiple_of(peer * cols, cols), cols)]
            copies[which].append(
                send(
                    part, dst.at[mine], ctx_send.at[which, step], ctx_recv.at[which, step],
                    (me_dp, peer),
                )
            )
    for which in (1, 2, 3):
        for copy in copies[which]:
            copy.start()
    stays = [pltpu.make_async_copy(weight, block(me_dp), local_sem.at[4])]
    stays.append(pltpu.make_async_copy(features, window.at[mine], local_sem.at[0]))
    for which, (src, dst) in enumerate(streams):
        part = src.at[:, pl.ds(pl.multiple_of(me_ctx * cols, cols), cols)]
        stays.append(pltpu.make_async_copy(part, dst.at[mine], local_sem.at[which + 1]))
    for copy in stays:
        copy.start()

    def arrived(index):
        push(block(index), index, right_send.at[0], me_dp).wait_recv()

    def relay(far):
        @pl.when(at - far >= 0)
        def _():
            index = me_dp - far * pair
            arrived(index)

            @pl.when(at + 1 < line)
            def _():
                push(block(index), index, right_send.at[at - far], me_dp + pair).start()

            others(index, block(index))

        @pl.when(at + far < line)
        def _():
            index = me_dp + far * pair
            arrived(index)

            @pl.when(at > 0)
            def _():
                push(block(index), index, left_send.at[at + far], me_dp - pair).start()

            others(index, block(index))

    steps = cols // LANES
    groups = LANES // group_width
    length = window.shape[0]
    clear(scratch, length, scratch[6].shape[1] // 2)

    def gradient_step(step, carry):
        lanes = lane_block(step)
        values_gradient(
            group_width, block_in.at[:, lanes], block_out.at[:, lanes], block_cot.at[:, lanes],
            taps.at[:, :, lanes], behind.at[group_rows(step, groups)], grad_values.at[:, lanes],
            scratch,
        )
        return carry

    def add_terms(index):
        part = pl.ds(pl.multiple_of(index * depth, depth), depth)
        terms[:, part] = lax.dot_general(
            grad_values[...], full[index], (((1,), (1,)), ((), ())), preferred_element_type=F32
        ).astype(BF16)

    def add_values(index):
        part = pl.ds(pl.multiple_of(index * depth, depth), depth)
        total[...] += jnp.dot(window[:, part], full[index], preferred_element_type=F32)

    if line > 1:
        relay(1)
    if pair == 2:
        arrived(at * pair + 1 - side)
    if halves:
        along_half().start()
    for which in (1, 2, 3):
        for copy in copies[which]:
            copy.wait()
    for copy in copies[0]:
        copy.start()
    for copy in stays:
        copy.wait()
    leaves = [
        pltpu.make_async_copy(src, dst, out_sem.at[which])
        for which, (src, dst) in enumerate(
            ((block_in, in_out), (block_out, out_out), (block_cot, cot_out), (window, window_out))
        )
    ]
    for leave in leaves[:3]:
        leave.start()
    total[...] = jnp.zeros_like(total)
    lax.fori_loop(0, steps // 2, gradient_step, 0)
    if line > 2:
        relay(2)
    lax.fori_loop(steps // 2, steps, gradient_step, 0)
    for far in range(3, line):
        relay(far)

    def near_terms(spot, carry):
        add_terms(spot * pair + side)
        return carry

    def near_values(spot, carry):
        add_values(spot * pair + side)
        return carry

    def far_both(step, carry):
        spot = lax.rem(at + step, line)
        index = spot * pair + 1 - side
        if halves:
            @pl.when(spot == buddy)
            def _():
                across_half(index).wait_recv()
                low = full.at[index, pl.ds(half, half)]
                send(low, low, half_send, half_recv, (buddy * pair + side, me_ctx)).wait_recv()

            pl.when((step > 0) & (spot != buddy))(lambda: arrived(index))
        else:
            pl.when(step > 0)(lambda: arrived(index))
        add_terms(index)
        add_values(index)
        return carry

    lax.fori_loop(0, line, near_terms, 0)
    for copy in copies[0]:
        copy.wait()
    leaves[3].start()
    lax.fori_loop(0, line, near_values, 0)
    if pair == 2:
        lax.fori_loop(0, line, far_both, 0)
    if halves:
        along_half().wait_send()
    values[...] = total[...].astype(BF16)
    for leave in leaves:
        leave.wait()
    for spot in range(line):
        if halves:
            pl.when(spot == buddy)(lambda spot=spot: across_half(spot * pair + side).wait_send())
            pl.when(spot != buddy)(
                lambda spot=spot: across(spot * pair + side, weight).wait_send()
            )
        elif pair == 2:
            across(spot * pair + side, weight).wait_send()

        @pl.when((at + 1 < line) & (spot <= at))
        def _():
            push(weight, me_dp, right_send.at[spot], me_dp).wait_send()

        @pl.when((at > 0) & (spot >= at))
        def _():
            push(weight, me_dp, left_send.at[spot], me_dp).wait_send()


def gather_all(dp, ctx, group_width, features, gate_in, gate_out, cot, weight, taps, behind):
    pair = 2 if dp % 2 == 0 else 1
    rows, channels = features.shape
    depth, cols = weight.shape
    length = rows * ctx
    span = behind.shape[1] // 2
    shapes = [(length, channels)] + [(length, cols)] * 5 + [(length, channels)]
    dma = pltpu.SemaphoreType.DMA
    line = dp // pair
    block = pltpu.VMEM((length, cols), BF16)
    return pl.pallas_call(
        functools.partial(gather_kernel, dp, ctx, pair, group_width),
        out_shape=[jax.ShapeDtypeStruct(shape, BF16) for shape in shapes],
        in_specs=[ANY] * 5 + [VMEM] * 2,
        out_specs=[ANY] * 4 + [VMEM] * 3,
        scratch_shapes=[
            pltpu.VMEM((length, channels), BF16), block, block, block,
            pltpu.VMEM((dp, depth, cols), BF16), pltpu.VMEM((length, cols), F32),
            dma((5,)), dma((4, ctx)), dma((4, ctx)), dma((line,)), dma((line,)), dma((line,)),
            dma((dp,)), dma((4,)), dma, dma,
        ]
        + mixer_scratch(length, span, group_width),
        compiler_params=pltpu.CompilerParams(
            collective_id=0, has_side_effects=True, vmem_limit_bytes=50 * 2**20
        ),
    )(features, gate_in, gate_out, cot, weight, taps, behind)


def scatter_kernel(
    dp, ctx, pair,
    group_width, row_scale, group_scale,
    window, grad_values, terms, gate_in, gate_out, values, cot, taps, ahead, behind,
    weight_out, features_out, layer_out, first_out, second_out, short_out, medium_out,
    held, from_pair, from_left, from_right, outgoing, from_buddy,
    terms_in, layer, first, second, short, medium, short_send, medium_send, short_in, medium_in,
    local_sem, buddy_send, buddy_recv, ctx_send, ctx_recv, small_send, small_recv,
    pair_send, pair_recv, right_send, left_recv, left_send, right_recv, out_sem,
    *scratch,
):
    me_dp, me_ctx = lax.axis_index("dp"), lax.axis_index("ctx")
    line = dp // pair
    at, side = me_dp // pair, lax.rem(me_dp, pair)
    rows, cols = layer_out.shape[0], layer.shape[1]
    depth = weight_out.shape[0]
    greet(dp, ctx)

    halves = pair == 2 and line % 2 == 0
    buddy = at + 1 - 2 * lax.rem(at, 2)
    half = depth // 2

    def make(index, target, spot):
        part = pl.ds(pl.multiple_of(index * depth, depth), depth)
        target[spot] = (
            lax.dot_general(
                window[:, part], grad_values[...], (((0,), (0,)), ((), ())),
                preferred_element_type=F32,
            )
            * row_scale
        ).astype(BF16)

    def swap_half(spot):
        top = pl.ds(0, half)
        return send(
            outgoing.at[spot, top], from_pair.at[spot, top], pair_send.at[spot],
            pair_recv.at[spot], (at * pair + 1 - side, me_ctx),
        )

    def to_buddy():
        return send(
            outgoing.at[buddy, pl.ds(half, half)], from_buddy, buddy_send, buddy_recv,
            (buddy * pair + side, me_ctx),
        )

    def swap(spot):
        return send(
            outgoing.at[spot], from_pair.at[spot], pair_send.at[spot],
            pair_recv.at[spot], (at * pair + 1 - side, me_ctx),
        )

    def to_right(spot):
        return send(
            held.at[spot], from_left.at[spot], right_send.at[spot], left_recv.at[spot],
            (me_dp + pair, me_ctx),
        )

    def to_left(spot):
        return send(
            held.at[spot], from_right.at[spot], left_send.at[spot], right_recv.at[spot],
            (me_dp - pair, me_ctx),
        )

    copies = {}
    mine = pl.ds(pl.multiple_of(me_ctx * cols, cols), cols)
    outs = ((layer, layer_out), (first, first_out), (second, second_out))
    for which, (src, dst) in enumerate(((terms, terms_in),) + outs):
        group = copies.setdefault(which, [])
        for step in range(1, ctx):
            peer = lax.rem(me_ctx + step, ctx)
            group.append(
                send(
                    src.at[pl.ds(pl.multiple_of(peer * rows, rows), rows)],
                    dst.at[me_ctx] if which == 0 else dst.at[:, mine],
                    ctx_send.at[which, step], ctx_recv.at[which, step], (me_dp, peer),
                )
            )
        part = src.at[pl.ds(pl.multiple_of(me_ctx * rows, rows), rows)]
        group.append(
            pltpu.make_async_copy(
                part, dst.at[me_ctx] if which == 0 else dst.at[:, mine], local_sem.at[which]
            )
        )
    group = copies.setdefault(4, [])
    for kind, (src, dst) in enumerate(((short_send, short_in), (medium_send, medium_in))):
        for step in range(1, dp):
            peer = lax.rem(me_dp + step, dp)
            group.append(
                send(
                    src, dst.at[me_dp], small_send.at[kind, step], small_recv.at[kind, step],
                    (peer, me_ctx),
                )
            )
        group.append(pltpu.make_async_copy(src, dst.at[me_dp], local_sem.at[4 + kind]))
    for copy in copies[0]:
        copy.start()
    span = 32

    def begin(step, carry):
        spot = at + (1 - 2 * lax.rem(step, 2)) * (line - 1 - step // 2)

        @pl.when((spot >= 0) & (spot < line))
        def _():
            if pair == 2:
                make(spot * pair + 1 - side, outgoing, spot)
            if halves:
                @pl.when(spot == buddy)
                def _():
                    swap_half(spot).start()
                    to_buddy().start()

                @pl.when(spot == at)
                def _():
                    to_buddy().wait_recv()

                    def join(row, carry):
                        part = pl.ds(pl.multiple_of(row * span, span), span)
                        low = pl.ds(pl.multiple_of(half + row * span, span), span)
                        outgoing[at, low] = (
                            outgoing[at, low].astype(F32) + from_buddy[part].astype(F32)
                        ).astype(BF16)
                        return carry

                    lax.fori_loop(0, half // span, join, 0)

                pl.when(spot != buddy)(lambda: swap(spot).start())
            elif pair == 2:
                swap(spot).start()
            make(spot * pair + side, held, spot)

        return carry

    lax.fori_loop(0, 2 * line - 1, begin, 0)
    steps = layer.shape[1] // LANES
    groups = LANES // group_width
    clear(scratch, layer.shape[0], scratch[6].shape[1] // 2)
    short[...] = jnp.zeros_like(short)

    def mixer_step(step, carry):
        lanes, owned = lane_block(step), group_rows(step, groups)
        mixer_block(
            group_width, gate_in.at[:, lanes], gate_out.at[:, lanes], values.at[:, lanes],
            cot.at[:, lanes], taps.at[:, :, lanes], ahead.at[owned], behind.at[owned],
            layer.at[:, lanes], first.at[:, lanes], second.at[:, lanes], short.at[:, lanes],
            medium.at[owned], scratch,
        )
        return carry

    def add(spot, source, count=depth):
        def body(step, carry):
            part = pl.ds(pl.multiple_of(step * span, span), span)
            held[spot, part] = (
                held[spot, part].astype(jnp.float32) + source[spot, part].astype(jnp.float32)
            ).astype(jnp.bfloat16)
            return carry

        lax.fori_loop(0, count // span, body, 0)

    def ready(spot):
        def whole():
            swap(spot).wait_recv()
            add(spot, from_pair)

        def part():
            swap_half(spot).wait_recv()
            add(spot, from_pair, half)

        if halves:
            pl.when(spot == buddy)(part)
            pl.when(spot != buddy)(whole)
        elif pair == 2:
            whole()

    def go_right(spot):
        ready(spot)

        @pl.when(at > 0)
        def _():
            to_right(spot).wait_recv()
            add(spot, from_left)

        to_right(spot).start()

    def go_left(spot):
        ready(spot)

        @pl.when(at + 1 < line)
        def _():
            to_left(spot).wait_recv()
            add(spot, from_right)

        to_left(spot).start()

    early = steps * 3 // 8
    lax.fori_loop(0, early, mixer_step, 0)
    for far in range(line - 1, 0, -1):
        pl.when(at + far < line)(functools.partial(go_right, at + far))
        pl.when(at - far >= 0)(functools.partial(go_left, at - far))
        if far == line - 1:
            lax.fori_loop(early, steps, mixer_step, 0)
            short_send[...] = (short[...] * row_scale).astype(BF16)
            medium_send[...] = (medium[...] * group_scale).astype(BF16)
            for which in (1, 2, 3, 4):
                for copy in copies[which]:
                    copy.start()
    for copy in copies[0]:
        copy.wait()

    def sum_terms(step, carry):
        part = pl.ds(pl.multiple_of(step * 16, 16), 16)
        summed = terms_in[0, part].astype(F32)
        for peer in range(1, ctx):
            summed = summed + terms_in[peer, part].astype(F32)
        features_out[part] = summed.astype(BF16)
        return carry

    lax.fori_loop(0, rows // 16, sum_terms, 0)
    for copy in copies[4]:
        copy.wait()
    summed = short_in[0].astype(F32)
    whole = medium_in[0].astype(F32)
    for peer in range(1, dp):
        summed = summed + short_in[peer].astype(F32)
        whole = whole + medium_in[peer].astype(F32)
    edge = short_out.shape[1]
    for index in range(3):
        short_out[index] = summed[8 * index : 8 * index + edge]
    medium_out[...] = whole
    ready(at)

    @pl.when(at > 0)
    def _():
        to_right(at).wait_recv()
        add(at, from_left)

    @pl.when(at + 1 < line)
    def _():
        to_left(at).wait_recv()
        add(at, from_right)

    result = pltpu.make_async_copy(held.at[at], weight_out, out_sem)
    result.start()
    for which in (1, 2, 3):
        for copy in copies[which]:
            copy.wait()
    for spot in range(line):
        if halves:
            pl.when(spot == buddy)(lambda spot=spot: swap_half(spot).wait_send())
            pl.when(spot != buddy)(lambda spot=spot: swap(spot).wait_send())
        elif pair == 2:
            swap(spot).wait_send()
        pl.when(spot > at)(lambda spot=spot: to_right(spot).wait_send())
        pl.when(spot < at)(lambda spot=spot: to_left(spot).wait_send())
    if halves:
        to_buddy().wait_send()
    result.wait()


def scatter_all(
    dp, ctx, group_width, row_scale, group_scale,
    window, grad_values, terms, gate_in, gate_out, values, cot, taps, ahead, behind,
):
    pair = 2 if dp % 2 == 0 else 1
    line = dp // pair
    length, cols = values.shape
    edge, span = taps.shape[1], ahead.shape[1] // 2
    group_count = ahead.shape[0]
    rows, channels, depth = length // ctx, terms.shape[1], window.shape[1] // dp
    shapes = [(depth, cols)] + [(rows, channels)] * 4
    dma = pltpu.SemaphoreType.DMA
    slots = pltpu.VMEM((line, depth, cols), BF16)
    block = pltpu.VMEM((length, cols), BF16)
    return pl.pallas_call(
        functools.partial(scatter_kernel, dp, ctx, pair, group_width, row_scale, group_scale),
        out_shape=[jax.ShapeDtypeStruct(shape, BF16) for shape in shapes]
        + [
            jax.ShapeDtypeStruct((3, edge, cols), F32),
            jax.ShapeDtypeStruct((group_count, span), F32),
        ],
        in_specs=[VMEM] * 2 + [ANY] + [VMEM] * 7,
        out_specs=[ANY, VMEM] + [ANY] * 3 + [VMEM] * 2,
        scratch_shapes=[slots] * 5
        + [pltpu.VMEM((depth // 2, cols), BF16)]
        + [
            pltpu.VMEM((ctx, rows, channels), BF16), block, block, block,
            pltpu.VMEM((32, cols), F32), pltpu.VMEM((group_count, span), F32),
            pltpu.VMEM((32, cols), BF16), pltpu.VMEM((group_count, span), BF16),
            pltpu.VMEM((dp, 32, cols), BF16), pltpu.VMEM((dp, group_count, span), BF16),
        ]
        + [dma((6,)), dma, dma, dma((4, ctx)), dma((4, ctx)), dma((2, dp)), dma((2, dp))]
        + [dma((line,))] * 6
        + [dma]
        + mixer_scratch(length, span, group_width),
        compiler_params=pltpu.CompilerParams(
            collective_id=1, has_side_effects=True, vmem_limit_bytes=50 * 2**20
        ),
    )(window, grad_values, terms, gate_in, gate_out, values, cot, taps, ahead, behind)


def local(features, gate_in, gate_out, value_weight, short_taps, medium_taps, cotangent):
    ctx = lax.axis_size("ctx")
    dp = lax.axis_size("dp")
    ctx_index = lax.axis_index("ctx")
    rows, channels = features.shape
    cols = value_weight.shape[1]
    span, group_count = medium_taps.shape
    group_width = channels // group_count
    total_rows = rows * ctx * dp
    row_scale = 1.0 / math.sqrt(total_rows)
    group_scale = 1.0 / math.sqrt(total_rows * group_width)
    taps = lax.dynamic_slice_in_dim(short_taps, ctx_index * cols, cols, 2)
    own_groups = group_count // ctx
    medium = lax.dynamic_slice_in_dim(medium_taps, ctx_index * own_groups, own_groups, 1)
    lifted = medium.astype(F32).T
    zeros = jnp.zeros((own_groups, span), F32)
    ahead = jnp.concatenate([zeros[:, :1], lifted[:, ::-1], zeros[:, 1:]], axis=1)
    behind = jnp.concatenate([lifted, zeros], axis=1)
    window, block_in, block_out, block_cot, values, grad_values, terms = gather_all(
        dp, ctx, group_width, features, gate_in, gate_out, cotangent, value_weight, taps, behind
    )
    weight_out, grad_features, layer_out, first_out, second_out, grad_short, grad_medium = (
        scatter_all(
            dp, ctx, group_width, row_scale, group_scale,
            window, grad_values, terms, block_in, block_out, values, block_cot, taps, ahead, behind,
        )
    )
    return (
        layer_out,
        grad_features,
        first_out,
        second_out,
        weight_out,
        grad_short,
        grad_medium[:, ::-1].T,
    )


def solution(mesh):
    rows, split = P(("dp", "ctx"), None), P("dp", "ctx")
    return jax.shard_map(
        local,
        mesh=mesh,
        in_specs=(rows, rows, rows, split, P(), P(), rows),
        out_specs=(rows, rows, rows, rows, split, P(None, None, "ctx"), P(None, "ctx")),
        check_vma=False,
    )
```
